32 devices in a mesh: dp: 8 (over y, x, core), fsdp: 4 (over z).
Axes of the slice: x: 2, y: 2, z: 4, core: 2. Of those that a mesh axis runs over, the one named last changes fastest.
Arguments:
- media: bfloat16 [32, 5, 256, 1024], P(('dp', 'fsdp')), may hold values from -6 to 6
- latents: bfloat16 [32, 5, 64, 1024], P(('dp', 'fsdp')), may hold values from -6 to 6
- counts: int32 [32], P(('dp', 'fsdp')), may hold values from 1 to 5
- cotangent: bfloat16 [32, 5, 64, 1024], P(('dp', 'fsdp')), may hold values from -6 to 6
- media_gain: float32 [1024], P(('dp', 'fsdp')), may hold values from 0.5 to 1.5
- media_bias: float32 [1024], P(('dp', 'fsdp')), may hold values from -1.5 to 1.5
- latent_gain: float32 [1024], P(('dp', 'fsdp')), may hold values from 0.5 to 1.5
- latent_bias: float32 [1024], P(('dp', 'fsdp')), may hold values from -1.5 to 1.5
- w_query: bfloat16 [1024, 512], P(('dp', 'fsdp')), may hold values from -0.1875 to 0.1875
- key_value_weight: bfloat16 [1024, 1024], P(('dp', 'fsdp')), may hold values from -0.1875 to 0.1875
- w_out: bfloat16 [512, 1024], P(('dp', 'fsdp')), may hold values from -2 to 2
- ff_gain: float32 [1024], P(('dp', 'fsdp')), may hold values from 0.3 to 3
- ff_bias: float32 [1024], P(('dp', 'fsdp')), may hold values from -4 to 4
- w_up: bfloat16 [1024, 4096], P(('dp', 'fsdp')), may hold values from -0.375 to 0.375
- contracting_projection_matrix: bfloat16 [4096, 1024], P(('dp', 'fsdp')), may hold values from -0.1875 to 0.1875
Outputs:
- latents_out: bfloat16 [32, 5, 64, 1024], P(('dp', 'fsdp'))
- media_grad: bfloat16 [32, 5, 256, 1024], P(('dp', 'fsdp'))
- latent_grad: float32 [32, 5, 64, 1024], P(('dp', 'fsdp'))
- grad_media_gain: float32 [1024], P(('dp', 'fsdp'))
- grad_media_bias: float32 [1024], P(('dp', 'fsdp'))
- grad_latent_gain: float32 [1024], P(('dp', 'fsdp'))
- grad_latent_bias: float32 [1024], P(('dp', 'fsdp'))
- grad_w_query: float32 [1024, 512], P(('dp', 'fsdp'))
- grad_w_keyval: float32 [1024, 1024], P(('dp', 'fsdp'))
- grad_w_out: float32 [512, 1024], P(('dp', 'fsdp'))
- grad_ff_gain: float32 [1024], P(('dp', 'fsdp'))
- grad_ff_bias: float32 [1024], P(('dp', 'fsdp'))
- grad_w_up: float32 [1024, 4096], P(('dp', 'fsdp'))
- grad_w_down: float32 [4096, 1024], P(('dp', 'fsdp'))
The draws below stay inside these ranges and needn't reach their ends.
Inputs may be any that keep to these rules, and one draw needn't show every extreme that they name: The first counts[s] of a sample's 5 image slots hold images; the rest are padding.
All inputs are finite; a program needn't handle non-finite values.
Results may differ from the reference program's by a relative error of at most 0.04.
Values may be sent and summed in bfloat16 or wider, within the bound.
No kernel may reach another device: no remote copies, remote signals or barrier semaphores. Data moves between devices by JAX's collectives and lax.ppermute only.
A program may use at most 192 MiB of HBM per device.

```python
import math
import jax
import jax.numpy as jnp
from jax import lax

D = 1024
HEADS = 8
HEAD = 64
FF = 4096
NL = 64
MT = 256
MAX_IMG = 5
INNER = 512
SAMPLES = 32


def place_ends(values, key, low, high):
    longest = values.shape.index(max(values.shape))
    spots = []
    for shift in (0, 1):
        where = [jax.random.randint(jax.random.fold_in(key, axis), (), 0, length) for axis, length in enumerate(values.shape)]
        where[longest] = (where[longest] + shift) % values.shape[longest]
        spots.append(tuple(where))
    return values.at[spots[0]].set(low).at[spots[1]].set(high)


def strengthened(values, own_key, source, target, parts, factor):
    def block_of(dim):
        return (jnp.arange(values.shape[dim]) // (values.shape[dim] // parts)).reshape((-1,) + (1,) * (values.ndim - 1 - dim))

    first = jax.random.permutation(own_key, parts)[block_of(target)]
    second = (block_of(target) + parts // 2) % parts
    return jnp.where((block_of(source) == first) | (block_of(source) == second), factor * values, values)


def levels(own_key, extent, cuts, low, largest):
    factor_of = 1.0
    for position, shards_of in cuts:
        draws = jax.random.uniform(jax.random.fold_in(jax.random.fold_in(own_key, 6), position), (shards_of,), jnp.float32, low / len(cuts), largest / len(cuts))
        factor_of = factor_of * jnp.repeat(jnp.exp(draws), extent[position] // shards_of).reshape((-1,) + (1,) * (len(extent) - 1 - position))
    return factor_of


def noise(stream_key, extent, scale, most, cuts=(), kind=jnp.bfloat16):
    array = jax.random.normal(stream_key, extent, jnp.float32) * scale
    if len(cuts) > 0:
        array = levels(stream_key, extent, cuts, -0.22, 0.18) * array
    return jnp.clip(array, min=-most, max=most).astype(kind)


def noise_with(own_key, extent, scale, bound, split, heavy, dtype=jnp.bfloat16):
    array = scale * jax.random.normal(own_key, extent, jnp.float32)
    if split:
        array = array * levels(own_key, extent, split, -0.22, 0.18)
    return jnp.clip(strengthened(array, jax.random.fold_in(own_key, 3), *heavy), -bound, bound).astype(dtype)


def setup_inputs(seed: int = 0) -> dict:
    seeds = jax.random.split(jax.random.key(seed), 16)
    return {
        "media": noise(seeds[0], (SAMPLES, MAX_IMG, MT, D), 1.0, 6.0, ((0, 32),)),
        "latents": noise(seeds[1], (SAMPLES, MAX_IMG, NL, D), 1.0, 6.0, ((0, 32),)),
        "counts": place_ends(jax.random.randint(seeds[2], (SAMPLES,), 1, MAX_IMG + 1), jax.random.fold_in(seeds[2], 1), 1, MAX_IMG).astype(jnp.int32),
        "cotangent": noise(seeds[3], (SAMPLES, MAX_IMG, NL, D), 1.0, 6.0, ((0, 32),)),
        "media_gain": jnp.clip(0.5 + 1.0 * jax.random.uniform(seeds[4], (D,), jnp.float32) ** levels(seeds[4], (D,), ((0, 32),), -0.2, 0.2), 0.5, 1.5),
        "media_bias": noise(seeds[5], (D,), 0.3, 1.5, ((0, 32),), jnp.float32),
        "latent_gain": jnp.clip(0.5 + 1.0 * jax.random.uniform(seeds[6], (D,), jnp.float32) ** levels(seeds[6], (D,), ((0, 32),), -0.2, 0.2), 0.5, 1.5),
        "latent_bias": noise(seeds[7], (D,), 0.3, 1.5, ((0, 32),), jnp.float32),
        "w_query": noise(seeds[8], (D, INNER), D ** -0.5, 0.1875, ((0, 32),)),
        "key_value_weight": noise(seeds[9], (D, 2 * INNER), D ** -0.5, 0.1875, ((0, 32),)),
        "w_out": noise(seeds[10], (INNER, D), (INNER // 64) ** -0.5, 2.0, ((0, 32),)),
        "ff_gain": jnp.clip(jnp.exp(math.log(3.0) - 2.3025851 * jax.random.uniform(seeds[11], (D,), jnp.float32) ** levels(seeds[11], (D,), ((0, 32),), -0.2, 0.2)), 0.3, 3.0),
        "ff_bias": noise(seeds[12], (D,), 1.0, 4.0, ((0, 32),), jnp.float32),
        "w_up": noise_with(seeds[13], (D, FF), D ** -0.5, 0.375, ((0, 32),), (0, 1, 32, 2.75)),
        "contracting_projection_matrix": noise_with(seeds[14], (FF, D), FF ** -0.5, 0.1875, ((0, 32),), (0, 1, 32, 2.75)),
    }


@jax.custom_vjp
def lower_precision_cast(v):
    return lax.optimization_barrier(v.astype(jnp.bfloat16)).astype(jnp.float32)

@jax.custom_vjp
def lower_precision_backward(v):
    return v

def low_keep(v):
    return (lower_precision_cast(v), None)

def low_pass(kept, grad):
    return (grad,)

def back_keep(v):
    return (v, None)

def back_low(kept, grad):
    return (lower_precision_cast(grad),)
lower_precision_cast.defvjp(low_keep, low_pass)
lower_precision_backward.defvjp(back_keep, back_low)
epsilon = 1e-05

def layer_norm(inputs, gain, bias):
    middle = lax.optimization_barrier(jnp.mean(inputs, -1, keepdims=True))
    centered = inputs - middle
    spread = lax.optimization_barrier(jnp.mean(centered * centered, -1, keepdims=True))
    return centered * lax.rsqrt(spread + epsilon) * gain + bias

def resampler(media_in, latent_in, mask_one, params):
    highest_precision = lax.Precision.HIGHEST
    media_gain, media_bias, latent_gain, latent_bias, w_query, key_value_weight, w_out, ff_gain, ff_bias, w_up, contracting_projection_matrix = params
    slots_here = latent_in.shape[0]
    key_rows = MT + NL
    media_norm = layer_norm(media_in, media_gain, media_bias)
    lat_norm = layer_norm(latent_in, latent_gain, latent_bias)
    lookup_feeding_matrix = lower_precision_cast(jnp.concatenate([media_norm, lat_norm], 1))
    lat_low = lookup_feeding_matrix[:, MT:]
    query = lower_precision_cast(lower_precision_backward(jnp.einsum('bnd,de->bne', lat_low, w_query, precision=highest_precision)))
    key_value_rows = lower_precision_cast(lower_precision_backward(jnp.einsum('owh,hx->owx', lookup_feeding_matrix, key_value_weight, precision=highest_precision)))
    query = query.reshape(slots_here, NL, HEADS, HEAD)
    keys = key_value_rows[..., :INNER].reshape(slots_here, key_rows, HEADS, HEAD)
    values = key_value_rows[..., INNER:].reshape(slots_here, key_rows, HEADS, HEAD)
    scores = lower_precision_backward(jnp.einsum('bnhc,bkhc->bhnk', query, keys, precision=highest_precision) * HEAD ** (-0.5))
    probs = lower_precision_cast(jax.nn.softmax(scores, -1))
    mixed = jnp.einsum('bhnk,bkhc->bnhc', probs, values, precision=highest_precision).reshape(slots_here, NL, INNER)
    mixed = lower_precision_cast(lower_precision_backward(mixed))
    attended = lower_precision_backward(jnp.einsum('bne,ed->bnd', mixed, w_out, precision=highest_precision))
    resid = latent_in + attended
    hid_low = lower_precision_cast(layer_norm(resid, ff_gain, ff_bias))
    pre_act = lower_precision_backward(jnp.einsum('bnd,df->bnf', hid_low, w_up, precision=highest_precision))
    act_low = lower_precision_cast(jax.nn.gelu(pre_act, approximate=False))
    branch = lower_precision_backward(jnp.einsum('bnf,fd->bnd', act_low, contracting_projection_matrix, precision=highest_precision))
    return (resid + branch) * mask_one[:, None, None]

def reference(media, latents, counts, cotangent, media_gain, media_bias, latent_gain, latent_bias, w_query, key_value_weight, w_out, ff_gain, ff_bias, w_up, contracting_projection_matrix):
    weights = tuple((tensor.astype(jnp.float32) for tensor in (media_gain, media_bias, latent_gain, latent_bias, w_query, key_value_weight, w_out, ff_gain, ff_bias, w_up, contracting_projection_matrix)))
    slot_mask = (jnp.arange(MAX_IMG)[None, :] < counts[:, None]).astype(jnp.float32)

    def sample_step(totals, element):
        media_one, latent_one, cot_one, mask_one = element

        def forward(media_in, latent_in, params):
            return resampler(media_in, latent_in, mask_one, params)
        result, backward = jax.vjp(forward, media_one.astype(jnp.float32), latent_one.astype(jnp.float32), weights)
        gradients = backward(cot_one.astype(jnp.float32))
        totals = jax.tree.map(jnp.add, totals, gradients[2])
        return (totals, (result.astype(jnp.bfloat16), gradients[0].astype(jnp.bfloat16), gradients[1]))
    initial = tuple((jnp.zeros_like(tensor) for tensor in weights))
    totals, stacked = lax.scan(sample_step, initial, (media, latents, cotangent, slot_mask))
    outputs, media_grad, latent_grad = stacked
    return (outputs, media_grad, latent_grad, totals[0], totals[1], totals[2], totals[3], totals[4], totals[5], totals[6], totals[7], totals[8], totals[9], totals[10])
```

```python
import jax
import jax.numpy as jnp
from jax import lax
from jax.sharding import PartitionSpec as P

HEAD = 64
AXES = ("dp", "fsdp")
LANES = 128
EPS = 1e-05
F32 = jnp.float32
BF16 = jnp.bfloat16


def log2_exact(count):
    bits = count.bit_length() - 1
    return bits if (1 << bits) == count else None


class Links:
    def __init__(self, mesh):
        dp_size, fsdp_size = mesh.shape["dp"], mesh.shape["fsdp"]
        self.total = dp_size * fsdp_size
        dp_bits, fsdp_bits = log2_exact(dp_size), log2_exact(fsdp_size)
        self.pairwise = dp_bits is not None and fsdp_bits is not None and dp_bits >= 1
        if self.pairwise:
            self.count = dp_bits + fsdp_bits
            inner = list(range(fsdp_bits))[::-1]
            last = [fsdp_bits]
            outer = list(range(fsdp_bits + 1, self.count))
            self.orders = (inner + outer + last, inner + outer[::-1] + last)

    def my_bit(self, bit):
        return (lax.axis_index(AXES) >> bit) & 1

    def swap(self, array, bit):
        pairs = [(i, i ^ (1 << bit)) for i in range(self.total)]
        return lax.ppermute(array, AXES, pairs)

    def gather(self, shard, order):
        if not self.pairwise:
            return lax.all_gather(shard, AXES, axis=0, tiled=True)
        held = []
        block = shard
        for bit in self.orders[order]:
            other = self.swap(block, bit)
            place = sum(1 for have in held if have > bit)
            mine = self.my_bit(bit)
            spot = lax.broadcasted_iota(jnp.int32, (2,) + (1,) * (block.ndim - place), 0)
            block = jnp.where(
                spot == mine, jnp.expand_dims(block, place), jnp.expand_dims(other, place)
            )
            held.append(bit)
        return block.reshape((self.total * shard.shape[0],) + shard.shape[1:])

    def scatter(self, product, rows, order):
        if not self.pairwise:
            return lax.psum_scatter(product(None), AXES, scatter_dimension=0, tiled=True)
        stages = self.orders[order][::-1]
        first = stages[0]
        mine = self.my_bit(first)
        left = [bit for bit in range(self.count)[::-1] if bit != first]
        width = rows // self.total
        away = product((first, 1 - mine))
        keep = product((first, mine))
        shape = (2,) * len(left) + (width,) + away.shape[1:]
        block = keep.astype(F32).reshape(shape) + self.swap(away, first).astype(F32).reshape(shape)
        for bit in stages[1:]:
            mine = self.my_bit(bit)
            place = left.index(bit)
            block = block.astype(BF16)
            away = lax.dynamic_index_in_dim(block, 1 - mine, place, keepdims=False)
            keep = lax.dynamic_index_in_dim(block, mine, place, keepdims=False)
            block = keep.astype(F32) + self.swap(away, bit).astype(F32)
            left.remove(bit)
        return block


def pick_columns(array, select, total):
    if select is None:
        return array
    bit, value = select
    rows, columns = array.shape
    low = (columns // total) << bit
    split = array.reshape(rows, columns // (2 * low), 2, low)
    return lax.dynamic_index_in_dim(split, value, 2, keepdims=False).reshape(rows, columns // 2)


def normalize(inputs):
    middle = jnp.mean(inputs, -1, keepdims=True)
    centered = inputs - middle
    inverse = lax.rsqrt(jnp.mean(centered * centered, -1, keepdims=True) + EPS)
    return centered * inverse, inverse


def norm_back(upstream, hat, inverse, gain):
    scaled = upstream * gain
    inner = (
        scaled
        - jnp.mean(scaled, -1, keepdims=True)
        - hat * jnp.mean(scaled * hat, -1, keepdims=True)
    )
    axes = tuple(range(upstream.ndim - 1))
    return inverse * inner, jnp.sum(upstream * hat, axis=axes), jnp.sum(upstream, axis=axes)


def exact_gelu(inputs):
    return jax.nn.gelu(inputs, approximate=False)


def matmul(left, right):
    return jnp.dot(left, right, preferred_element_type=F32)


def matmul_nt(left, right):
    return lax.dot_general(left, right, (((1,), (1,)), ((), ())), preferred_element_type=F32)


def matmul_tn(left, right):
    return lax.dot_general(left, right, (((0,), (0,)), ((), ())), preferred_element_type=F32)


def on_device(links, media, latents, counts, cotangent, media_gain, media_bias, latent_gain,
              latent_bias, w_query, key_value_weight, w_out, ff_gain, ff_bias, w_up, w_down):
    total = links.total
    samples, slots_each, media_rows, width = media.shape
    latent_rows = latents.shape[2]
    slots = samples * slots_each
    key_rows = media_rows + latent_rows
    inner_width = w_query.shape[1]
    heads = inner_width // HEAD
    score_scale = HEAD ** (-0.5)
    live = (jnp.arange(slots_each)[None, :] < counts[:, None]).astype(F32).reshape(slots, 1, 1)

    vectors = jnp.stack(
        [media_gain, media_bias, latent_gain, latent_bias, ff_gain, ff_bias], 1
    ).astype(BF16)
    vectors = jnp.pad(vectors, ((0, 0), (0, LANES - vectors.shape[1])))
    kv_w = links.gather(key_value_weight, 0)
    query_w = links.gather(jnp.concatenate([w_query, vectors], 1), 1)
    out_w = links.gather(w_out, 1)
    up_w = links.gather(w_up, 0)
    down_w = links.gather(w_down, 1)
    vectors = query_w[:, inner_width : inner_width + 6].astype(F32).T
    query_w = query_w[:, :inner_width]
    media_gain, media_bias, latent_gain, latent_bias, ff_gain, ff_bias = vectors

    media_flat = media.reshape(slots, media_rows, width)
    lat_full = latents.reshape(slots, latent_rows, width).astype(F32)
    media_hat, media_inv = normalize(media_flat.astype(F32))
    lat_hat, lat_inv = normalize(lat_full)
    media_norm = (media_hat * media_gain + media_bias).astype(BF16)
    lat_norm = (lat_hat * latent_gain + latent_bias).astype(BF16)
    key_input = jnp.concatenate([media_norm, lat_norm], 1).reshape(slots * key_rows, width)
    lat_low = lat_norm.reshape(slots * latent_rows, width)
    query = matmul(lat_low, query_w).astype(BF16)
    query = query.reshape(slots, latent_rows, heads, HEAD)
    keyval = matmul(key_input, kv_w).astype(BF16).reshape(slots, key_rows, 2 * inner_width)
    keys = keyval[..., :inner_width].reshape(slots, key_rows, heads, HEAD)
    values = keyval[..., inner_width:].reshape(slots, key_rows, heads, HEAD)
    scores = jnp.einsum("bnhc,bkhc->bhnk", query, keys, preferred_element_type=F32) * score_scale
    probs = jax.nn.softmax(scores, -1)
    probs_low = probs.astype(BF16)
    mixed = jnp.einsum("bhnk,bkhc->bnhc", probs_low, values, preferred_element_type=F32)
    mixed = mixed.reshape(slots * latent_rows, inner_width).astype(BF16)
    resid = lat_full + matmul(mixed, out_w).reshape(lat_full.shape)

    hid_hat, hid_inv = normalize(resid)
    hid_low = (hid_hat * ff_gain + ff_bias).astype(BF16).reshape(slots * latent_rows, width)
    pre_act = matmul(hid_low, up_w)
    act, gelu_back = jax.vjp(exact_gelu, pre_act)
    act_low = act.astype(BF16)
    grad_out = cotangent.reshape(lat_full.shape).astype(F32) * live
    grad_low = grad_out.astype(BF16).reshape(slots * latent_rows, width)

    def weight_grad(left, right):
        return lambda select: matmul_tn(pick_columns(left, select, total), right).astype(BF16)

    g_down = links.scatter(weight_grad(act_low, grad_low), act_low.shape[1], 1)
    branch = matmul(act_low, down_w).reshape(lat_full.shape)
    latents_out = ((resid + branch) * live).astype(BF16).reshape(latents.shape)

    grad_act = matmul_nt(grad_low, down_w)
    grad_pre = gelu_back(grad_act)[0].astype(BF16)
    g_up = links.scatter(weight_grad(hid_low, grad_pre), width, 0)
    grad_hid = matmul_nt(grad_pre, up_w).reshape(lat_full.shape)
    grad_norm_in, g_ff_gain, g_ff_bias = norm_back(grad_hid, hid_hat, hid_inv, ff_gain)
    grad_resid = grad_out + grad_norm_in
    resid_low = grad_resid.astype(BF16).reshape(slots * latent_rows, width)

    g_out = links.scatter(weight_grad(mixed, resid_low), inner_width, 1)
    grad_mixed = matmul_nt(resid_low, out_w).astype(BF16)
    grad_mixed = grad_mixed.reshape(slots, latent_rows, heads, HEAD)
    grad_values = jnp.einsum("bhnk,bnhc->bkhc", probs_low, grad_mixed, preferred_element_type=F32)
    grad_probs = jnp.einsum("bnhc,bkhc->bhnk", grad_mixed, values, preferred_element_type=F32)
    grad_scores = probs * (grad_probs - jnp.sum(probs * grad_probs, -1, keepdims=True))
    grad_scores = grad_scores.astype(BF16)
    grad_query = jnp.einsum("bhnk,bkhc->bnhc", grad_scores, keys, preferred_element_type=F32)
    grad_query = (grad_query * score_scale).reshape(slots * latent_rows, inner_width).astype(BF16)
    grad_keys = jnp.einsum("bhnk,bnhc->bkhc", grad_scores, query, preferred_element_type=F32)
    grad_keyval = jnp.concatenate(
        [
            (grad_keys * score_scale).astype(BF16).reshape(slots * key_rows, inner_width),
            grad_values.astype(BF16).reshape(slots * key_rows, inner_width),
        ],
        -1,
    )
    g_kv = links.scatter(weight_grad(key_input, grad_keyval), width, 0)
    grad_input = matmul_nt(grad_keyval, kv_w).reshape(slots, key_rows, width)
    grad_latnorm = (
        matmul_nt(grad_query, query_w).reshape(lat_full.shape) + grad_input[:, media_rows:]
    )
    grad_lat_in, g_lat_gain, g_lat_bias = norm_back(grad_latnorm, lat_hat, lat_inv, latent_gain)
    grad_media, g_media_gain, g_media_bias = norm_back(
        grad_input[:, :media_rows], media_hat, media_inv, media_gain
    )
    g_vectors = jnp.stack(
        [g_media_gain, g_media_bias, g_lat_gain, g_lat_bias, g_ff_gain, g_ff_bias], 0
    )
    g_vectors = jnp.pad(g_vectors, ((0, LANES - g_vectors.shape[0]), (0, 0)))

    def query_grad(select):
        weights = matmul_tn(pick_columns(lat_low, select, total), grad_query)
        return jnp.concatenate([weights, pick_columns(g_vectors, select, total).T], 1).astype(BF16)

    g_query = links.scatter(query_grad, width, 1)
    g_vectors = g_query[:, inner_width : inner_width + 6]
    return (
        latents_out,
        grad_media.astype(BF16).reshape(media.shape),
        (grad_resid + grad_lat_in).reshape(latents.shape),
        g_vectors[:, 0].astype(F32),
        g_vectors[:, 1].astype(F32),
        g_vectors[:, 2].astype(F32),
        g_vectors[:, 3].astype(F32),
        g_query[:, :inner_width].astype(F32),
        g_kv.astype(F32),
        g_out.astype(F32),
        g_vectors[:, 4].astype(F32),
        g_vectors[:, 5].astype(F32),
        g_up.astype(F32),
        g_down.astype(F32),
    )


def solution(mesh):
    links = Links(mesh)

    def body(*arrays):
        return on_device(links, *arrays)

    def rows(ndim):
        return P(AXES, *([None] * (ndim - 1)))

    return jax.shard_map(
        body,
        mesh=mesh,
        in_specs=tuple(rows(n) for n in (4, 4, 1, 4, 1, 1, 1, 1, 2, 2, 2, 1, 1, 2, 2)),
        out_specs=tuple(rows(n) for n in (4, 4, 4, 1, 1, 1, 1, 2, 2, 2, 1, 1, 2, 2)),
        check_vma=False,
    )
```
